32 devices in a mesh: gx: 4 (over z), gy: 8 (over y, x, core).
Axes of the slice: x: 2, y: 2, z: 4, core: 2. Of those that a mesh axis runs over, the one named last changes fastest.
Arguments:
- velocity: float32 [128, 256, 3, 256], P('gx', 'gy'), may hold values from -6 to 6
- fiber_loads: float32 [3, 49152], P(None, ('gx', 'gy')), may hold values from -96 to 96
- fractions: float32 [3, 49152], P(None, ('gx', 'gy')), may hold values from 0 to 1
- corners: int32 [3, 49152], P(None, ('gx', 'gy')), may hold values from 0 to 255, as said below
- neighbours: int32 [49152], P(('gx', 'gy')), may hold values from 0 to 1535
- counts: int32 [1024], P(('gx', 'gy')), may hold values from 1 to 48, as said below
Outputs:
- velocity_next: float32 [128, 256, 3, 256], P('gx', 'gy')
- fiber_velocity: float32 [3, 49152], P(None, ('gx', 'gy'))
The draws below stay inside these ranges and needn't reach their ends.
Inputs may be any that keep to these rules, and one draw needn't show every extreme that they name: `counts`: in every draw some destination device receives 48 live slots from every source device. For a slot whose destination device has x block a and y block b: corners[0] is a * 32 + o mod 128 with o from -2 to 30, corners[1] is b * 32 + o mod 256 with o from -2 to 30, corners[2] any cell along z.
All inputs are finite; a program needn't handle non-finite values.
Results may differ from the reference program's by a relative error of at most 0.0029.
Values may be sent and summed in bfloat16 or wider, within the bound.
No kernel may reach another device: no remote copies, remote signals or barrier semaphores. Data moves between devices by JAX's collectives and lax.ppermute only.
A program may use at most 128 MiB of HBM per device.

```python
import jax
import jax.numpy as jnp
from jax import lax

CX = 32
CY = 32
NZ = 256
CAP = 48
NX = 128
NY = 256
SLOTS = 49152
N_GX = 4
N_GY = 8


def draw_counts(key, part):
    devices = N_GX * N_GY
    first, second = jax.random.split(jax.random.fold_in(key, 11))
    table = jax.random.randint(first, (devices, devices), 1, CAP + 1)
    chosen = jax.random.randint(second, (), 0, devices)
    table = jnp.where(jnp.arange(devices)[None, :] == chosen, CAP, table)
    return table.reshape(-1).astype(jnp.int32)


def draw_corners(key, part):
    devices = N_GX * N_GY
    total = devices * devices * CAP
    first, second, third = jax.random.split(jax.random.fold_in(key, 23), 3)
    slot_ids = jnp.arange(total, dtype=jnp.int32)
    target = slot_ids // CAP % devices
    block_x = target // N_GY
    block_y = target % N_GY
    corner_x = (block_x * CX + jax.random.randint(first, (total,), -2, CX - 1)) % NX
    corner_y = (block_y * CY + jax.random.randint(second, (total,), -2, CY - 1)) % NY
    corner_z = jax.random.randint(third, (total,), 0, NZ)
    return jnp.stack([corner_x, corner_y, corner_z]).astype(jnp.int32)


def set_ends(values, rng, smallest, high):
    longest = values.shape.index(max(values.shape))
    spots = []
    for shift in (0, 1):
        where = [jax.random.randint(jax.random.fold_in(rng, axis), (), 0, length) for axis, length in enumerate(values.shape)]
        where[longest] = (where[longest] + shift) % values.shape[longest]
        spots.append(tuple(where))
    return values.at[spots[0]].set(smallest).at[spots[1]].set(high)


def shard_levels(stream_key, shape, cuts, least, largest):
    loudness = 1.0
    for dim, shards_of in cuts:
        heights = jax.random.uniform(jax.random.fold_in(jax.random.fold_in(stream_key, 6), dim), (shards_of,), jnp.float32, least / len(cuts), largest / len(cuts))
        loudness = loudness * jnp.repeat(jnp.exp(heights), shape[dim] // shards_of).reshape((-1,) + (1,) * (len(shape) - 1 - dim))
    return loudness


def bell_draw(own_key, shape, deviation, limit, cuts=(), held_as=jnp.bfloat16):
    entries = jax.random.normal(own_key, shape, jnp.float32) * deviation
    if len(cuts) > 0:
        entries = shard_levels(own_key, shape, cuts, -0.22, 0.18) * entries
    return jnp.clip(entries, min=-limit, max=limit).astype(held_as)


def setup_inputs(seed: int = 0) -> dict:
    key_list = jax.random.split(jax.random.key(seed), 7)
    velocity = bell_draw(key_list[0], (NX, NY, 3, NZ), 1.0, 6.0, ((0, 4), (1, 8)), jnp.float32)
    fiber_loads = bell_draw(key_list[1], (3, SLOTS), 16.0, 96.0, ((1, 32),), jnp.float32)
    fractions = jnp.clip(1.0 * jax.random.uniform(key_list[2], (3, SLOTS), jnp.float32) ** shard_levels(key_list[2], (3, SLOTS), ((1, 32),), -0.2, 0.2), 0.0, 1.0)
    corners = draw_corners(jax.random.fold_in(key_list[6], 71), 0)
    neighbours = set_ends(jax.random.randint(key_list[4], (SLOTS,), 0, CAP * N_GX * N_GY), jax.random.fold_in(key_list[4], 1), 0, (CAP * N_GX * N_GY) - 1).astype(jnp.int32)
    counts = draw_counts(jax.random.fold_in(key_list[6], 71), 0)
    return dict(velocity=velocity, fiber_loads=fiber_loads, fractions=fractions, corners=corners, neighbours=neighbours, counts=counts)


viscosity = 0.15


def peskin(fraction):
    nodes = jnp.arange(4, dtype=jnp.float32).reshape((4,) + (1,) * fraction.ndim)
    return 0.25 * (1.0 + jnp.cos(0.5 * jnp.pi * (1.0 + fraction[None] - nodes)))


def laplace_of(field):
    result = jnp.roll(field, -1, 0) + jnp.roll(field, 1, 0)
    result = result + jnp.roll(field, -1, 1) + jnp.roll(field, 1, 1)
    result = result + jnp.roll(field, -1, 3) + jnp.roll(field, 1, 3)
    return result - 6.0 * field


def to_bf16(values):
    return lax.optimization_barrier(values.astype(jnp.bfloat16)).astype(jnp.float32)


def reference(velocity, fiber_loads, fractions, corners, neighbours, counts):
    devices = N_GX * N_GY
    total = devices * devices * CAP
    slot_ids = jnp.arange(total, dtype=jnp.int32)
    live_mask = (jnp.arange(CAP, dtype=jnp.int32)[None, :] < counts[:, None]).reshape(-1).astype(jnp.float32)
    position = corners.astype(jnp.float32) + fractions
    owner_base = (slot_ids // (devices * CAP)) * (devices * CAP)
    partner = (owner_base + neighbours).astype(jnp.int32)
    stiffness = jnp.array([2.0 / NX, 2.0 / NY, 2.0 / NZ], jnp.float32)[:, None]
    forcing = (fiber_loads + stiffness * (position[:, partner] - position)) * live_mask
    weight_x = peskin(fractions[0])
    weight_y = peskin(fractions[1])
    weight_z = peskin(fractions[2])
    component = jnp.arange(3, dtype=jnp.int32)

    def place(offset):
        step_i = offset // 16
        step_j = (offset // 4) % 4
        step_k = offset % 4
        cell_x = (corners[0] + step_i) % NX
        cell_y = (corners[1] + step_j) % NY
        cell_z = (corners[2] + step_k) % NZ
        plane_wts = to_bf16(weight_x[step_i] * weight_y[step_j])
        return cell_x, cell_y, cell_z, plane_wts, weight_z[step_k]

    def spread_step(grid_sum, offset):
        cell_x, cell_y, cell_z, plane_wts, depth_wts = place(offset)
        push_rows = to_bf16(forcing * depth_wts[None, :])
        values = plane_wts[None, :] * push_rows
        grid_sum = grid_sum.at[cell_x[None, :], cell_y[None, :], component[:, None], cell_z[None, :]].add(values)
        return grid_sum, None

    grid_sum, _ = lax.scan(spread_step, jnp.zeros((NX, NY, 3, NZ), jnp.float32), jnp.arange(64, dtype=jnp.int32))
    field = velocity + grid_sum
    for sweep in range(2):
        field = field + viscosity * laplace_of(field)
    rounded = to_bf16(field)

    def gather_step(running, offset):
        cell_x, cell_y, cell_z, plane_wts, depth_wts = place(offset)
        picked = rounded[cell_x[:, None], cell_y[:, None], component[None, :], cell_z[:, None]].T
        return running + plane_wts[None, :] * picked * depth_wts[None, :], None

    running, _ = lax.scan(gather_step, jnp.zeros((3, total), jnp.float32), jnp.arange(64, dtype=jnp.int32))
    return field, running * live_mask
```

```python
import functools

import jax
import jax.numpy as jnp
from jax import lax
from jax.experimental import pallas as pl
from jax.experimental.pallas import tpu as pltpu
from jax.sharding import PartitionSpec as P

viscosity = 0.15
F32 = jnp.float32
BF16 = jnp.bfloat16
LANES = 128
REACH = 4

SIDES = ((-1, -1), (-1, 0), (-1, 1), (1, -1), (1, 0), (1, 1), (0, -1), (0, 1))


def iota(shape, dim):
    return lax.broadcasted_iota(jnp.int32, shape, dim)


def piece_at(tile_of, start, width, target):
    first, off = divmod(start, LANES)
    shift = (target - off) % LANES
    out = pltpu.roll(tile_of(first), shift, 1) if shift else tile_of(first)
    spill = off + width - LANES
    if spill > 0:
        rest = tile_of(first + 1)
        rest = pltpu.roll(rest, shift, 1) if shift else rest
        lane = iota(out.shape, 1)
        begin = (target + width - spill) % LANES
        end = begin + spill
        inside = (lane >= begin) & (lane < end)
        if end > LANES:
            inside = inside | (lane < end - LANES)
        out = jnp.where(inside, rest, out)
    return out


def lane_mask(shape, begin, end):
    lane = iota(shape, 1)
    return (lane >= begin) & (lane < end)


def front_kernel(dims, counts, loads, fractions, corners, neighbours, out, rows, buckets):
    groups_x, groups_y, cells_x, cells_y, cells_z, per_peer = dims
    devices = groups_x * groups_y
    slots = loads.shape[1]
    tiles = slots // LANES
    whole_x, whole_y = groups_x * cells_x, groups_y * cells_y
    position = corners[...].astype(F32) + fractions[...]
    for c in range(3):
        rows[2 * c : 2 * c + 1, :] = loads[c : c + 1, :]
        rows[2 * c + 1 : 2 * c + 2, :] = position[c : c + 1, :]
    rows[6:8, :] = jnp.zeros((2, slots), F32)
    sub = iota((8, LANES), 0)
    lane = iota((8, LANES), 1)
    even = (sub % 2) == 0
    stiffness = jnp.where(sub == 1, 2.0 / whole_x, jnp.where(sub == 3, 2.0 / whole_y, 2.0 / cells_z))
    stiffness = jnp.where((sub % 2 == 1) & (sub < 6), stiffness, 0.0).astype(F32)

    def force(t, _):
        at = pl.ds(pl.multiple_of(t * LANES, LANES), LANES)
        index = jnp.broadcast_to(neighbours[0:1, at], (8, LANES))
        high, low = index // LANES, index % LANES
        here = rows[:, at]
        partner = jnp.zeros((8, LANES), F32)
        for h in range(tiles):
            picked = jnp.take_along_axis(rows[:, h * LANES : (h + 1) * LANES], low, axis=1)
            partner = jnp.where(high == h, picked, partner)
        pull = pltpu.roll(stiffness * (partner - here), 7, 0)
        rows[:, at] = jnp.where(even, here + pull, here)
        return 0

    lax.fori_loop(0, tiles, force, 0)

    period = jnp.where(sub == 1, float(whole_x), jnp.where(sub == 3, float(whole_y), 4.0e9)).astype(F32)
    for d in range(devices):
        a, b = divmod(d, groups_y)
        got = piece_at(lambda i: rows[:, i * LANES : (i + 1) * LANES], d * per_peer, per_peer, 0)
        base = jnp.where(sub == 1, float(a * cells_x), jnp.where(sub == 3, float(b * cells_y), 0.0)).astype(F32)
        moved = got - base
        moved = jnp.where(moved > 0.5 * period, moved - period, moved)
        moved = jnp.where(moved < -0.5 * period, moved + period, moved)
        live = lane < counts[d]
        buckets[d] = jnp.where(even, jnp.where(live, got, 0.0), moved)

    tiles_out = out.shape[2] // LANES

    def send(d, _):
        a, b = d // groups_y, d % groups_y
        acc = [jnp.zeros((8, LANES), F32) for _ in range(tiles_out)]

        def put(value, start, rows_ok):
            m, off = divmod(start, LANES)
            value = pltpu.roll(value, off, 1) if off else value
            ok = lane_mask((8, LANES), off, min(off + per_peer, LANES))
            ok = ok if rows_ok is None else ok & rows_ok
            acc[m] = jnp.where(ok, value, acc[m])
            if off + per_peer > LANES:
                ok = lane_mask((8, LANES), 0, off + per_peer - LANES)
                ok = ok if rows_ok is None else ok & rows_ok
                acc[m + 1] = jnp.where(ok, value, acc[m + 1])

        for k, (dx, dy) in enumerate(SIDES):
            owner = ((a + dx + groups_x) % groups_x) * groups_y + (b + dy + groups_y) % groups_y
            put(buckets[owner], k * per_peer, None)
        own = buckets[d]
        for c in range(3):
            put(pltpu.roll(own, 6 - 2 * c, 0), c * per_peer, sub >= 6)
        for m in range(tiles_out):
            out[d, :, m * LANES : (m + 1) * LANES] = acc[m]
        return 0

    lax.fori_loop(0, devices, send, 0)


def quarter_sine(t):
    half_pi = 1.5707963267948966
    coeffs = []
    term = half_pi
    for n in range(8):
        coeffs.append(term)
        term = -term * half_pi * half_pi / ((2 * n + 2) * (2 * n + 3))
    square = t * t
    total = jnp.full_like(t, coeffs[-1])
    for coeff in coeffs[-2::-1]:
        total = total * square + coeff
    return total * t


def main_kernel(
    dims, got, velocity, x_low, x_high, y_low, y_high, field, back,
    lists, floors, sines, cosines, wts, push, depth, side_wts, grid, mid, rounded, own_vel, values, sem_in, sem_out,
):
    groups_x, groups_y, cells_x, cells_y, cells_z, per_peer = dims
    sources = groups_x * groups_y
    points = sources * per_peer
    block = wts.shape[1]
    blocks = points // block
    ext_x, ext_y = cells_x + 2 * REACH, cells_y + 2 * REACH
    inner_x = cells_x + REACH
    load_vel = pltpu.make_async_copy(velocity, own_vel, sem_in)
    load_vel.start()
    sub = iota((8, LANES), 0)

    for k in range(len(SIDES) + 1):
        for m in range(points // LANES):
            acc = jnp.zeros((8, LANES), F32)
            for s in range(m * LANES // per_peer, -(-(m + 1) * LANES // per_peer)):
                at = s * per_peer - m * LANES
                ok = lane_mask((8, LANES), max(at, 0), min(at + per_peer, LANES))
                tile_of = lambda i, s=s: got[s, :, i * LANES : (i + 1) * LANES]
                if k < len(SIDES):
                    acc = jnp.where(ok, piece_at(tile_of, k * per_peer, per_peer, at % LANES), acc)
                else:
                    for c in range(3):
                        value = piece_at(tile_of, c * per_peer, per_peer, at % LANES)
                        value = pltpu.roll(value, (2 * c - 6) % 8, 0)
                        acc = jnp.where(ok & (sub // 2 == c), value, acc)
            lists[k, :, m * LANES : (m + 1) * LANES] = acc
        position = lists[k]
        floor = jnp.floor(position)
        fraction = position - floor
        floors[k] = floor
        sines[k] = quarter_sine(fraction)
        cosines[k] = quarter_sine(1.0 - fraction)

    def weights(k, c, at):
        row = slice(2 * c + 1, 2 * c + 2)
        s, co = sines[k, row, at], cosines[k, row, at]
        return (0.25 * (1.0 - s), 0.25 * (1.0 + co), 0.25 * (1.0 + s), 0.25 * (1.0 - co))

    def table(coordinate, cells, wt):
        out = jnp.zeros(jnp.broadcast_shapes(coordinate.shape, cells[0].shape), F32)
        for cell, w in zip(cells, wt):
            out = jnp.where(coordinate == cell, w, out)
        return out

    def coord(rows, lanes, f):
        return f(iota((rows, lanes), 0)).astype(F32)

    def along_x(k, at, lanes, first, count, shift):
        cell = floors[k, 1:2, at] + float(shift)
        rows = -(-count // 8) * 8
        return table(coord(rows, lanes, lambda r: r + first), [cell + float(i) for i in range(4)], weights(k, 0, at))

    def along_y(k, at, lanes, rows, rule, shift):
        cell = floors[k, 3:4, at] + float(shift)
        return table(coord(rows, lanes, rule), [cell + float(i) for i in range(4)], weights(k, 1, at))

    def push_rows(k, at, to, lanes, keep):
        cell = floors[k, 5:6, at]
        cells = []
        for i in range(4):
            moved = cell + float(i)
            cells.append(jnp.where(moved >= float(cells_z), moved - float(cells_z), moved))
        step = 64
        wt = weights(k, 2, at)
        for z in range(0, cells_z, step):
            part = table(coord(step, lanes, lambda r: r + z), cells, wt)
            if keep:
                depth[z : z + step, to] = part
            for c in range(3):
                force = lists[k, 2 * c : 2 * c + 1, at]
                push[c, z : z + step, to] = (part * force).astype(BF16)

    chunk = 256

    def circle(r):
        return jnp.where(r < cells_y + REACH, r, r - ext_y)

    def build_own(base):
        def step(i, _):
            at = pl.ds(pl.multiple_of(base + i * chunk, chunk), chunk)
            to = pl.ds(pl.multiple_of(i * chunk, chunk), chunk)
            k = len(SIDES)
            ax = along_x(k, at, chunk, -2, inner_x, 0)
            ay = along_y(k, at, chunk, ext_y, circle, 0)
            for x in range(0, inner_x, 2):
                pair = jnp.concatenate([ax[x : x + 1] * ay, ax[x + 1 : x + 2] * ay], axis=0)
                wts[x * ext_y : (x + 2) * ext_y, to] = pair.astype(BF16)
            push_rows(k, at, to, chunk, True)
            return 0

        lax.fori_loop(0, block // chunk, step, 0)

    def dot_t(a, b):
        return lax.dot_general(a, b, (((1,), (1,)), ((), ())), preferred_element_type=F32)

    for base in range(0, points, block):
        build_own(base)

        def spread_own(c, _, base=base):
            total = dot_t(wts[...], push[c]).reshape(inner_x, ext_y, cells_z)
            if base == 0:
                grid[2 : 2 + inner_x, c] = total
                grid[0:2, c] = jnp.zeros((2, ext_y, cells_z), F32)
                grid[2 + inner_x :, c] = jnp.zeros((2, ext_y, cells_z), F32)
            else:
                grid[2 : 2 + inner_x, c] += total
            return 0

        lax.fori_loop(0, 3, spread_own, 0)

    edge = REACH + 2
    for k, (dx, dy) in enumerate(SIDES):
        for base in range(0, points, block):
            first = -REACH if dx < 0 else cells_x - 2
            tile_a = 0 if dy < 0 else cells_y - 8

            def step(i, _, k=k, dx=dx, dy=dy, base=base, first=first, tile_a=tile_a):
                at = pl.ds(pl.multiple_of(base + i * chunk, chunk), chunk)
                to = pl.ds(pl.multiple_of(i * chunk, chunk), chunk)
                if dx:
                    ax = along_x(k, at, chunk, first, edge, dx * cells_x)
                    ay = along_y(k, at, chunk, ext_y, circle, dy * cells_y)
                    for x in range(0, edge, 2):
                        pair = jnp.concatenate([ax[x : x + 1] * ay, ax[x + 1 : x + 2] * ay], axis=0)
                        side_wts[x * ext_y : (x + 2) * ext_y, to] = pair.astype(BF16)
                else:
                    ax = along_x(k, at, chunk, -2, inner_x, 0)
                    rule = lambda r: circle(jnp.where(r < 8, r + tile_a, r - 8 + cells_y))
                    ay = along_y(k, at, chunk, 16, rule, dy * cells_y)
                    for x in range(inner_x):
                        side_wts[x * 16 : (x + 1) * 16, to] = (ax[x : x + 1] * ay).astype(BF16)
                push_rows(k, at, to, chunk, False)
                return 0

            lax.fori_loop(0, block // chunk, step, 0)

            def spread(c, _, dx=dx, first=first, tile_a=tile_a):
                if dx:
                    total = dot_t(side_wts[0 : edge * ext_y, :], push[c]).reshape(edge, ext_y, cells_z)
                    grid[first + REACH : first + REACH + edge, c] += total
                else:
                    total = dot_t(side_wts[...], push[c]).reshape(inner_x, 2, 8, cells_z)
                    grid[2 : 2 + inner_x, c, tile_a : tile_a + 8] += total[:, 0]
                    grid[2 : 2 + inner_x, c, cells_y : cells_y + 8] += total[:, 1]
                return 0

            lax.fori_loop(0, 3, spread, 0)

    load_vel.wait()

    def add_velocity(x, _):
        for c in range(3):
            grid[x + REACH, c, 0:cells_y] += own_vel[x, c]
        return 0

    lax.fori_loop(0, cells_x, add_velocity, 0)

    def add_edges(x, _):
        for c in range(3):
            grid[x, c, 0:cells_y] += x_low[x, c].astype(F32)
            grid[x + REACH + cells_x, c, 0:cells_y] += x_high[x, c].astype(F32)
        return 0

    lax.fori_loop(0, REACH, add_edges, 0)

    def add_sides(x, _):
        for c in range(3):
            pair = jnp.concatenate([y_high[x, c].astype(F32), y_low[x, c].astype(F32)], axis=0)
            grid[x, c, cells_y:ext_y] += pair
        return 0

    lax.fori_loop(0, ext_x, add_sides, 0)

    def swept(ref, x, c):
        center = ref[x, c]
        total = ref[x - 1, c] + ref[x + 1, c]
        total = total + pltpu.roll(center, 1, 0) + pltpu.roll(center, ext_y - 1, 0)
        total = total + pltpu.roll(center, 1, 1) + pltpu.roll(center, cells_z - 1, 1)
        return center + viscosity * (total - 6.0 * center)

    def first_sweep(x, _):
        for c in range(3):
            mid[x, c] = swept(grid, x, c)
        return 0

    lax.fori_loop(1, ext_x - 1, first_sweep, 0)

    def second_sweep(i, _):
        for c in range(3):
            two = [swept(mid, 2 + 2 * i, c), swept(mid, 3 + 2 * i, c)]
            grid[2 + 2 * i, c] = two[0]
            grid[3 + 2 * i, c] = two[1]
            at = pl.ds(pl.multiple_of(i * 2 * ext_y, 2 * ext_y), 2 * ext_y)
            rounded[c, at, :] = jnp.concatenate(two, axis=0).astype(BF16)
        return 0

    lax.fori_loop(0, inner_x // 2, second_sweep, 0)
    store = pltpu.make_async_copy(grid.at[REACH : REACH + cells_x, :, 0:cells_y, :], field, sem_out)
    store.start()

    values[3:8, :] = jnp.zeros((5, points), F32)
    for base in range(0, points, block):
        if blocks > 1:
            build_own(base)
        for c in range(3):
            mixed = lax.dot_general(rounded[c], wts[...], (((0,), (0,)), ((), ())), preferred_element_type=F32)
            values[c : c + 1, base : base + block] = jnp.sum(mixed * depth[...], axis=0, keepdims=True)
    for s in range(sources):
        back[s] = piece_at(lambda i: values[:, i * LANES : (i + 1) * LANES], s * per_peer, per_peer, 0)
    store.wait()


def last_kernel(per_peer, counts, got, out):
    devices = got.shape[0]
    for m in range(out.shape[1] // LANES):
        acc = jnp.zeros((8, LANES), F32)
        for s in range(m * LANES // per_peer, -(-(m + 1) * LANES // per_peer)):
            at = s * per_peer - m * LANES
            lane = iota((8, LANES), 1)
            ok = (lane >= max(at, 0)) & (lane < jnp.minimum(at + counts[s], min(at + per_peer, LANES)))
            value = got[s]
            value = pltpu.roll(value, at % LANES, 1) if at % LANES else value
            acc = jnp.where(ok, value, acc)
        out[:, m * LANES : (m + 1) * LANES] = acc[0:3]


def body(velocity, fiber_loads, fractions, corners, neighbours, counts):
    groups_x = lax.axis_size("gx")
    groups_y = lax.axis_size("gy")
    devices = groups_x * groups_y
    slots = fiber_loads.shape[1]
    per_peer = slots // devices
    cells_x, cells_y, cells_z = (velocity.shape[0], velocity.shape[1], velocity.shape[3])
    dims = (groups_x, groups_y, cells_x, cells_y, cells_z, per_peer)
    both = ("gx", "gy")
    width = -(-len(SIDES) * per_peer // LANES) * LANES
    vmem = pl.BlockSpec(memory_space=pltpu.VMEM)
    smem = pl.BlockSpec(memory_space=pltpu.SMEM)
    hbm = pl.BlockSpec(memory_space=pl.ANY)

    payload = pl.pallas_call(
        functools.partial(front_kernel, dims),
        out_shape=jax.ShapeDtypeStruct((devices, 8, width), F32),
        in_specs=[smem] + [vmem] * 4,
        out_specs=vmem,
        scratch_shapes=[pltpu.VMEM((8, slots), F32), pltpu.VMEM((devices, 8, LANES), F32)],
        name="points_out",
    )(counts, fiber_loads, fractions, corners, neighbours.reshape(1, slots))
    received = lax.all_to_all(payload, both, split_axis=0, concat_axis=0, tiled=True)

    stored = jnp.transpose(velocity, (0, 2, 1, 3))

    def shifted(low_part, high_part, axis):
        peers = lax.axis_size(axis)
        up = [(i, (i + 1) % peers) for i in range(peers)]
        down = [(j, i) for i, j in up]
        return lax.ppermute(high_part, axis, up), lax.ppermute(low_part, axis, down)

    x_first = stored[:REACH].astype(BF16)
    x_last = stored[cells_x - REACH :].astype(BF16)
    x_low, x_high = shifted(x_first, x_last, "gx")
    y_first = jnp.concatenate([x_low[:, :, :REACH], stored[:, :, :REACH].astype(BF16), x_high[:, :, :REACH]], 0)
    y_last = jnp.concatenate(
        [x_low[:, :, cells_y - REACH :], stored[:, :, cells_y - REACH :].astype(BF16), x_high[:, :, cells_y - REACH :]], 0
    )
    y_low, y_high = shifted(y_first, y_last, "gy")

    block = min(slots, 1536)
    ext_x, ext_y, inner_x = cells_x + 2 * REACH, cells_y + 2 * REACH, cells_x + REACH
    lists = len(SIDES) + 1
    side_rows = max((REACH + 2) * ext_y, inner_x * 16)
    field, back = pl.pallas_call(
        functools.partial(main_kernel, dims),
        out_shape=(
            jax.ShapeDtypeStruct(stored.shape, F32),
            jax.ShapeDtypeStruct((devices, 8, LANES), F32),
        ),
        in_specs=[vmem, hbm] + [vmem] * 4,
        out_specs=(hbm, vmem),
        scratch_shapes=[
            pltpu.VMEM((lists, 8, slots), F32),
            pltpu.VMEM((lists, 8, slots), F32),
            pltpu.VMEM((lists, 8, slots), F32),
            pltpu.VMEM((lists, 8, slots), F32),
            pltpu.VMEM((inner_x * ext_y, block), BF16),
            pltpu.VMEM((3, cells_z, block), BF16),
            pltpu.VMEM((cells_z, block), F32),
            pltpu.VMEM((side_rows, block), BF16),
            pltpu.VMEM((ext_x, 3, ext_y, cells_z), F32),
            pltpu.VMEM((ext_x, 3, ext_y, cells_z), F32),
            pltpu.VMEM((3, inner_x * ext_y, cells_z), BF16),
            pltpu.VMEM(stored.shape, F32),
            pltpu.VMEM((8, slots), F32),
            pltpu.SemaphoreType.DMA(()),
            pltpu.SemaphoreType.DMA(()),
        ],
        compiler_params=pltpu.CompilerParams(vmem_limit_bytes=52 * 1024 * 1024),
        name="step",
    )(received, stored, x_low, x_high, y_low, y_high)
    returned = lax.all_to_all(back, both, split_axis=0, concat_axis=0, tiled=True)
    sampled = pl.pallas_call(
        functools.partial(last_kernel, per_peer),
        out_shape=jax.ShapeDtypeStruct((3, slots), F32),
        in_specs=[smem, vmem],
        out_specs=vmem,
        name="points_back",
    )(counts, returned)
    return (jnp.transpose(field, (0, 2, 1, 3)), sampled)


def solution(mesh):
    return jax.shard_map(
        body,
        mesh=mesh,
        in_specs=(
            P("gx", "gy", None, None),
            P(None, ("gx", "gy")),
            P(None, ("gx", "gy")),
            P(None, ("gx", "gy")),
            P(("gx", "gy")),
            P(("gx", "gy")),
        ),
        out_specs=(P("gx", "gy", None, None), P(None, ("gx", "gy"))),
        check_vma=False,
    )
```

```python
import functools

import jax
import jax.numpy as jnp
from jax import lax
from jax.experimental import pallas as pl
from jax.experimental.pallas import tpu as pltpu
from jax.sharding import PartitionSpec as P


viscosity = 0.15
F32 = jnp.float32
BF16 = jnp.bfloat16
LANES = 128
MIB = 1024 * 1024
STEP_MIB = 58
REACH = 4

SIDES = ((-1, -1), (-1, 0), (-1, 1), (1, -1), (1, 0), (1, 1), (0, -1), (0, 1))


def iota(shape, dim):
    return lax.broadcasted_iota(jnp.int32, shape, dim)


def piece_at(tile_of, start, width, target):
    first, off = divmod(start, LANES)
    shift = (target - off) % LANES
    out = pltpu.roll(tile_of(first), shift, 1) if shift else tile_of(first)
    spill = off + width - LANES
    if spill > 0:
        rest = tile_of(first + 1)
        rest = pltpu.roll(rest, shift, 1) if shift else rest
        lane = iota(out.shape, 1)
        begin = (target + width - spill) % LANES
        end = begin + spill
        inside = (lane >= begin) & (lane < end)
        if end > LANES:
            inside = inside | (lane < end - LANES)
        out = jnp.where(inside, rest, out)
    return out


def lane_mask(shape, begin, end):
    lane = iota(shape, 1)
    return (lane >= begin) & (lane < end)


def front_kernel(dims, counts, loads, fractions, corners, neighbours, out, rows, buckets, reach, order):
    groups_x, groups_y, cells_x, cells_y, cells_z, per_peer = dims
    devices = groups_x * groups_y
    slots = loads.shape[1]
    tiles = slots // LANES
    whole_x, whole_y = groups_x * cells_x, groups_y * cells_y
    position = corners[...].astype(F32) + fractions[...]
    for c in range(3):
        rows[2 * c : 2 * c + 1, :] = loads[c : c + 1, :]
        rows[2 * c + 1 : 2 * c + 2, :] = position[c : c + 1, :]
    rows[6:8, :] = jnp.zeros((2, slots), F32)
    sub = iota((8, LANES), 0)
    lane = iota((8, LANES), 1)
    even = (sub % 2) == 0
    stiffness = jnp.where(sub == 1, 2.0 / whole_x, jnp.where(sub == 3, 2.0 / whole_y, 2.0 / cells_z))
    stiffness = jnp.where((sub % 2 == 1) & (sub < 6), stiffness, 0.0).astype(F32)

    def force(t, _):
        at = pl.ds(pl.multiple_of(t * LANES, LANES), LANES)
        index = jnp.broadcast_to(neighbours[at].reshape(1, LANES), (8, LANES))
        high, low = index // LANES, index % LANES
        here = rows[:, at]
        partner = jnp.zeros((8, LANES), F32)
        for h in range(tiles):
            picked = jnp.take_along_axis(rows[:, h * LANES : (h + 1) * LANES], low, axis=1)
            partner = jnp.where(high == h, picked, partner)
        pull = pltpu.roll(stiffness * (partner - here), 7, 0)
        rows[:, at] = jnp.where(even, here + pull, here)
        return 0

    lax.fori_loop(0, tiles, force, 0, unroll=4)

    far = 1.0e9
    low_x = sum([jnp.where(sub == k, cells_x - REACH - 3.0 if dx < 0 else -far, 0.0) for k, (dx, _) in enumerate(SIDES)])
    end_x = sum([jnp.where(sub == k, float(REACH) if dx > 0 else far, 0.0) for k, (dx, _) in enumerate(SIDES)])
    low_y = sum([jnp.where(sub == k, cells_y - REACH - 3.0 if dy < 0 else -far, 0.0) for k, (_, dy) in enumerate(SIDES)])
    end_y = sum([jnp.where(sub == k, float(REACH) if dy > 0 else far, 0.0) for k, (_, dy) in enumerate(SIDES)])
    period = jnp.where(sub == 1, float(whole_x), jnp.where(sub == 3, float(whole_y), 4.0e9)).astype(F32)
    for d in range(devices):
        a, b = divmod(d, groups_y)
        got = piece_at(lambda i: rows[:, i * LANES : (i + 1) * LANES], d * per_peer, per_peer, 0)
        base = jnp.where(sub == 1, float(a * cells_x), jnp.where(sub == 3, float(b * cells_y), 0.0)).astype(F32)
        moved = got - base
        moved = jnp.where(moved > 0.5 * period, moved - period, moved)
        moved = jnp.where(moved < -0.5 * period, moved + period, moved)
        live = lane < counts[d]
        local = jnp.where(live, jnp.where(even, got, moved), jnp.where(even | (lane >= per_peer), 0.0, moved))
        buckets[d] = local
        at_x = jnp.broadcast_to(local[1:2], (8, LANES))
        at_y = jnp.broadcast_to(local[3:4], (8, LANES))
        near = live & (at_x >= low_x) & (at_x < end_x) & (at_y >= low_y) & (at_y < end_y)
        reach[8 * d : 8 * d + 8, :] = jnp.where(near, 1.0, 0.0)

    before = jnp.where(iota((LANES, LANES), 0) <= iota((LANES, LANES), 1), 1.0, 0.0).astype(BF16)
    reach[...] = jnp.dot(reach[...].astype(BF16), before, preferred_element_type=F32)
    starts = sum([jnp.where(sub == k, (k * per_peer) % LANES, 0) for k in range(len(SIDES))])
    rank = ((lane - starts + LANES) % LANES).astype(F32)

    def find(d, _):
        upto = reach[pl.ds(pl.multiple_of(8 * d, 8), 8), :]
        spot = jnp.zeros((8, LANES), jnp.int32)
        for bit in (32, 16, 8, 4, 2, 1):
            seen = jnp.take_along_axis(upto, spot + (bit - 1), axis=1)
            spot = jnp.where(seen <= rank, spot + bit, spot)
        order[d] = spot
        return 0

    lax.fori_loop(0, devices, find, 0, unroll=16)
    tiles_out = out.shape[2] // LANES

    def send(d):
        a, b = divmod(d, groups_y)
        acc = [jnp.zeros((8, LANES), F32) for _ in range(tiles_out)]

        def put(value, start, rows_ok):
            m, off = divmod(start, LANES)
            ok = lane_mask((8, LANES), off, min(off + per_peer, LANES))
            ok = ok if rows_ok is None else ok & rows_ok
            acc[m] = jnp.where(ok, value, acc[m])
            if off + per_peer > LANES:
                ok = lane_mask((8, LANES), 0, off + per_peer - LANES)
                ok = ok if rows_ok is None else ok & rows_ok
                acc[m + 1] = jnp.where(ok, value, acc[m + 1])

        counted = []
        for k, (dx, dy) in enumerate(SIDES):
            owner = ((a + dx + groups_x) % groups_x) * groups_y + (b + dy + groups_y) % groups_y
            index = jnp.broadcast_to(order[owner, k : k + 1, :], (8, LANES))
            put(jnp.take_along_axis(buckets[owner], index, axis=1), k * per_peer, None)
            counted.append(jnp.broadcast_to(reach[8 * owner + k : 8 * owner + k + 1, :], (8, LANES)))
        own = buckets[d]
        for c in range(3):
            value = pltpu.roll(own, 6 - 2 * c, 0)
            value = pltpu.roll(value, (c * per_peer) % LANES, 1) if c else value
            put(value, c * per_peer, sub >= 6)
        for k, count in enumerate(counted):
            acc[-1] = jnp.where((sub == 7) & (lane == LANES - 8 + k), count, acc[-1])
        for m in range(tiles_out):
            out[d, :, m * LANES : (m + 1) * LANES] = acc[m]

    for d in range(devices):
        send(d)


def quarter_sine(t):
    half_pi = 1.5707963267948966
    coeffs = []
    term = half_pi
    for n in range(8):
        coeffs.append(term)
        term = -term * half_pi * half_pi / ((2 * n + 2) * (2 * n + 3))
    square = t * t
    total = jnp.full_like(t, coeffs[-1])
    for coeff in coeffs[-2::-1]:
        total = total * square + coeff
    return total * t


def main_kernel(
    dims, got, velocity, x_low_in, x_high_in, y_low_in, y_high_in, field, back,
    own, floors, sines, cosines, wts, push, depth, side_wts, side_push, grid, mid, rounded, own_vel, values, x_sides, y_sides, sems,
):
    groups_x, groups_y, cells_x, cells_y, cells_z, per_peer = dims
    sources = groups_x * groups_y
    points = sources * per_peer
    block = wts.shape[1]
    blocks = points // block
    ext_x, ext_y = cells_x + 2 * REACH, cells_y + 2 * REACH
    inner_x = cells_x + REACH
    load_vel = pltpu.make_async_copy(velocity, own_vel, sems.at[0])
    load_vel.start()
    load_sides = []
    for i, ref in enumerate((x_low_in, x_high_in, y_low_in, y_high_in)):
        to = (x_sides if i < 2 else y_sides).at[i % 2]
        load_sides.append(pltpu.make_async_copy(ref, to, sems.at[2 + i]))
        load_sides[-1].start()
    sub = iota((8, LANES), 0)
    lane = iota((8, LANES), 1)

    for m in range(points // LANES):
        acc = jnp.zeros((8, LANES), F32)
        for s in range(m * LANES // per_peer, -(-(m + 1) * LANES // per_peer)):
            at = s * per_peer - m * LANES
            ok = lane_mask((8, LANES), max(at, 0), min(at + per_peer, LANES))
            for c in range(3):
                value = piece_at(lambda i, s=s: got[s, :, i * LANES : (i + 1) * LANES], c * per_peer, per_peer, at % LANES)
                value = pltpu.roll(value, (2 * c - 6) % 8, 0)
                acc = jnp.where(ok & (sub // 2 == c), value, acc)
        own[:, m * LANES : (m + 1) * LANES] = acc

    def split(position):
        floor = jnp.floor(position)
        fraction = position - floor
        return floor, quarter_sine(fraction), quarter_sine(1.0 - fraction)

    floors[...], sines[...], cosines[...] = split(own[...])

    def weights(s, co):
        return (0.25 * (1.0 - s), 0.25 * (1.0 + co), 0.25 * (1.0 + s), 0.25 * (1.0 - co))

    def table(coordinate, cells, wt):
        out = jnp.zeros(jnp.broadcast_shapes(coordinate.shape, cells[0].shape), F32)
        for cell, w in zip(cells, wt):
            out = jnp.where(coordinate == cell, w, out)
        return out

    def coord(rows, lanes, f):
        return f(iota((rows, lanes), 0)).astype(F32)

    def along(cell, wt, rows, rule):
        return table(coord(rows, cell.shape[1], rule), [cell + float(i) for i in range(4)], wt)

    def push_rows(cell, wt, forces, to_push, to, keep):
        lanes = cell.shape[1]
        cells = []
        for i in range(4):
            moved = cell + float(i)
            cells.append(jnp.where(moved >= float(cells_z), moved - float(cells_z), moved))
        step = 64
        for z in range(0, cells_z, step):
            part = table(coord(step, lanes, lambda r: r + z), cells, wt)
            if keep:
                depth[z : z + step, to] = part
            for c in range(3):
                to_push[c, z : z + step, to] = (part * forces[c]).astype(BF16)

    def circle(r):
        return jnp.where(r < cells_y + REACH, r, r - ext_y)

    def pair_rows(ax, ay, x):
        return jnp.concatenate([ax[x : x + 1] * ay, ax[x + 1 : x + 2] * ay], axis=0).astype(BF16)

    chunk = 256

    def build_own(base):
        def step(i, _):
            at = pl.ds(pl.multiple_of(base + i * chunk, chunk), chunk)
            to = pl.ds(pl.multiple_of(i * chunk, chunk), chunk)
            cell = [floors[2 * c + 1 : 2 * c + 2, at] for c in range(3)]
            wt = [weights(sines[2 * c + 1 : 2 * c + 2, at], cosines[2 * c + 1 : 2 * c + 2, at]) for c in range(3)]
            ax = along(cell[0], wt[0], -(-inner_x // 8) * 8, lambda r: r - 2)
            ay = along(cell[1], wt[1], ext_y, circle)
            for x in range(0, inner_x, 2):
                wts[x * ext_y : (x + 2) * ext_y, to] = pair_rows(ax, ay, x)
            push_rows(cell[2], wt[2], [own[2 * c : 2 * c + 1, at] for c in range(3)], push, to, True)
            return 0

        lax.fori_loop(0, block // chunk, step, 0)

    def dot_t(a, b):
        return lax.dot_general(a, b, (((1,), (1,)), ((), ())), preferred_element_type=F32)

    for base in range(0, points, block):
        build_own(base)
        if base == 0:
            load_vel.wait()

        def spread_own(c, _, base=base):
            total = dot_t(wts[...], push[c]).reshape(inner_x, ext_y, cells_z)
            if base == 0:
                grid[2 : 2 + inner_x, c] = total
                grid[0:2, c] = jnp.zeros((2, ext_y, cells_z), F32)
                grid[2 + inner_x :, c] = jnp.zeros((2, ext_y, cells_z), F32)
                grid[REACH : REACH + cells_x, c, 0:cells_y] = total[2 : 2 + cells_x, 0:cells_y] + own_vel[:, c]
            else:
                grid[2 : 2 + inner_x, c] += total
            return 0

        lax.fori_loop(0, 3, spread_own, 0)

    edge = REACH + 2
    together = chunk // 8
    rounds = sources // together
    most = got[0, :, got.shape[2] - LANES :]
    for s in range(1, sources):
        most = jnp.maximum(most, got[s, :, got.shape[2] - LANES :])
    counts = [
        jnp.max(jnp.where((sub == 7) & (lane == LANES - 8 + k), most, 0.0)).astype(jnp.int32) for k in range(len(SIDES))
    ]

    def side(it, slot, k):
        dx, dy = SIDES[k]
        first = -REACH if dx < 0 else cells_x - 2
        tile_a = 0 if dy < 0 else cells_y - 8
        start = k * per_peer + (it // rounds if rounds > 1 else it) * 8
        source = (it % rounds if rounds > 1 else 0) * together
        at = pl.ds(pl.multiple_of(start // LANES * LANES, LANES), LANES)
        off = start % LANES
        parts = []
        for m in range(chunk // LANES):
            acc = jnp.zeros((8, LANES), F32)
            for i in range(LANES // 8):
                value = pltpu.roll(got[source + m * (LANES // 8) + i, :, at], (8 * i - off + LANES) % LANES, 1)
                acc = jnp.where(lane // 8 == i, value, acc)
            parts.append(acc)
        data = jnp.concatenate(parts, axis=1)
        floor, sine, cosine = split(data)
        cell = [floor[2 * c + 1 : 2 * c + 2] for c in range(3)]
        cell[0] = cell[0] + float(dx * cells_x)
        cell[1] = cell[1] + float(dy * cells_y)
        wt = [weights(sine[2 * c + 1 : 2 * c + 2], cosine[2 * c + 1 : 2 * c + 2]) for c in range(3)]
        if dx:
            ax = along(cell[0], wt[0], 8, lambda r: r + first)
            ay = along(cell[1], wt[1], ext_y, circle)
            for x in range(0, edge, 2):
                side_wts[slot, x * ext_y : (x + 2) * ext_y, :] = pair_rows(ax, ay, x)
        else:
            ax = along(cell[0], wt[0], -(-inner_x // 8) * 8, lambda r: r - 2)
            ay = along(cell[1], wt[1], 16, lambda r: circle(jnp.where(r < 8, r + tile_a, r - 8 + cells_y)))
            for x in range(inner_x):
                side_wts[slot, x * 16 : (x + 1) * 16, :] = (ax[x : x + 1] * ay).astype(BF16)
        push_rows(cell[2], wt[2], [data[2 * c : 2 * c + 1] for c in range(3)], side_push.at[slot], slice(None), False)

    def side_sum(slot, k):
        dx, dy = SIDES[k]
        first = -REACH if dx < 0 else cells_x - 2
        tile_a = 0 if dy < 0 else cells_y - 8
        for c in range(3):
            if dx:
                total = dot_t(side_wts[slot, 0 : edge * ext_y, :], side_push[slot, c]).reshape(edge, ext_y, cells_z)
                grid[first + REACH : first + REACH + edge, c] += total
            else:
                total = dot_t(side_wts[slot, 0 : inner_x * 16, :], side_push[slot, c]).reshape(inner_x, 2, 8, cells_z)
                grid[2 : 2 + inner_x, c, tile_a : tile_a + 8] += total[:, 0]
                grid[2 : 2 + inner_x, c, cells_y : cells_y + 8] += total[:, 1]

    for pair in (SIDES.index((dx, dy)) for dx, dy in SIDES if dx < 0 or (dx == 0 and dy < 0)):
        other = SIDES.index((-SIDES[pair][0], SIDES[pair][1] if SIDES[pair][0] else -SIDES[pair][1]))

        def both(it, _, pair=pair, other=other):
            side(it, 0, pair)
            side(it, 1, other)
            side_sum(0, pair)
            side_sum(1, other)
            return 0

        lax.fori_loop(0, (jnp.maximum(counts[pair], counts[other]) + 7) // 8 * rounds, both, 0)

    for copy in load_sides:
        copy.wait()
    (x_low, x_high), (y_low, y_high) = (x_sides.at[0], x_sides.at[1]), (y_sides.at[0], y_sides.at[1])

    def add_edges(x, _):
        for c in range(3):
            grid[x, c, 0:cells_y] += x_low[x, c].astype(F32)
            grid[x + REACH + cells_x, c, 0:cells_y] += x_high[x, c].astype(F32)
        return 0

    lax.fori_loop(0, REACH, add_edges, 0)

    def add_sides(x, _):
        for c in range(3):
            pair = jnp.concatenate([y_high[x, c].astype(F32), y_low[x, c].astype(F32)], axis=0)
            grid[x, c, cells_y:ext_y] += pair
        return 0

    lax.fori_loop(0, ext_x, add_sides, 0, unroll=2)

    center_wt = (1.0 - 6.0 * viscosity) / viscosity

    eight = iota((8, cells_z), 0)

    def swept(ref, x, c):
        tiles = [ref[x, c, i : i + 8, :] for i in range(0, ext_y, 8)]
        ups = [pltpu.roll(tile, 1, 0) for tile in tiles]
        downs = [pltpu.roll(tile, 7, 0) for tile in tiles]
        out = []
        for i, tile in enumerate(tiles):
            at = slice(8 * i, 8 * i + 8)
            total = ref[x - 1, c, at, :] + ref[x + 1, c, at, :]
            total = total + jnp.where(eight == 0, ups[i - 1], ups[i])
            total = total + jnp.where(eight == 7, downs[(i + 1) % len(tiles)], downs[i])
            total = total + pltpu.roll(tile, 1, 1) + pltpu.roll(tile, cells_z - 1, 1)
            out.append(center_wt * tile + total)
        return jnp.concatenate(out, axis=0)

    def first_sweep(i, _):
        for x in range(4):
            for c in range(3):
                mid[1 + 4 * i + x, c] = swept(grid, 1 + 4 * i + x, c)
        return 0

    lax.fori_loop(0, (ext_x - 2) // 4, first_sweep, 0)
    for x in range((ext_x - 2) // 4 * 4 + 1, ext_x - 1):
        for c in range(3):
            mid[x, c] = swept(grid, x, c)

    def second_sweep(i, _):
        for j in range(2):
            at_x = 2 + 4 * i + 2 * j
            for c in range(3):
                two = [viscosity * viscosity * swept(mid, at_x + x, c) for x in range(2)]
                grid[at_x, c] = two[0]
                grid[at_x + 1, c] = two[1]
                at = pl.ds(pl.multiple_of((2 * i + j) * 2 * ext_y, 2 * ext_y), 2 * ext_y)
                rounded[c, at, :] = jnp.concatenate(two, axis=0).astype(BF16)
        return 0

    lax.fori_loop(0, inner_x // 4, second_sweep, 0)
    store = pltpu.make_async_copy(grid.at[REACH : REACH + cells_x, :, 0:cells_y, :], field, sems.at[1])
    store.start()

    values[3:8, :] = jnp.zeros((5, points), F32)
    for base in range(0, points, block):
        if blocks > 1:
            build_own(base)
        for c in range(3):
            mixed = lax.dot_general(rounded[c], wts[...], (((0,), (0,)), ((), ())), preferred_element_type=F32)
            values[c : c + 1, base : base + block] = jnp.sum(mixed * depth[...], axis=0, keepdims=True)
    for s in range(sources):
        back[s] = piece_at(lambda i: values[:, i * LANES : (i + 1) * LANES], s * per_peer, per_peer, 0)
    store.wait()


def edge_kernel_x(stored, out_first, out_last, held, sems):
    cells_x = stored.shape[0]
    copies = []
    for i, at in enumerate((0, cells_x - REACH)):
        copies.append(pltpu.make_async_copy(stored.at[at : at + REACH], held.at[i], sems.at[i]))
        copies[-1].start()
    for i, out in enumerate((out_first, out_last)):
        copies[i].wait()
        out[...] = held[i].astype(BF16)


def edge_kernel_y(stored, x_low, x_high, out_first, out_last, held, sides, sems):
    cells_x, cells_y = stored.shape[0], stored.shape[2]
    copies = []
    for i, at in enumerate((0, cells_y - 8)):
        copies.append(pltpu.make_async_copy(stored.at[:, :, at : at + 8, :], held.at[i], sems.at[i]))
    for i, ref in enumerate((x_low, x_high)):
        copies.append(pltpu.make_async_copy(ref, sides.at[i], sems.at[2 + i]))
    for copy in copies:
        copy.start()
    for copy in copies:
        copy.wait()
    out_first[REACH : REACH + cells_x] = held[0, :, :, 0:REACH].astype(BF16)
    out_last[REACH : REACH + cells_x] = held[1, :, :, 8 - REACH :].astype(BF16)
    for i, at in enumerate((0, REACH + cells_x)):
        out_first[at : at + REACH] = sides[i, :, :, 0:8].astype(F32)[:, :, 0:REACH].astype(BF16)
        out_last[at : at + REACH] = sides[i, :, :, cells_y - 8 :].astype(F32)[:, :, 8 - REACH :].astype(BF16)


def last_kernel(per_peer, counts, got, out):
    for m in range(out.shape[1] // LANES):
        acc = jnp.zeros((8, LANES), F32)
        for s in range(m * LANES // per_peer, -(-(m + 1) * LANES // per_peer)):
            at = s * per_peer - m * LANES
            lane = iota((8, LANES), 1)
            ok = (lane >= max(at, 0)) & (lane < jnp.minimum(at + counts[s], min(at + per_peer, LANES)))
            value = got[s]
            value = pltpu.roll(value, at % LANES, 1) if at % LANES else value
            acc = jnp.where(ok, value, acc)
        out[:, m * LANES : (m + 1) * LANES] = acc[0:3]


def staged(velocity, fiber_loads, fractions, corners, neighbours, counts):
    groups_x = lax.axis_size("gx")
    groups_y = lax.axis_size("gy")
    devices = groups_x * groups_y
    slots = fiber_loads.shape[1]
    per_peer = slots // devices
    cells_x, cells_y, cells_z = (velocity.shape[0], velocity.shape[1], velocity.shape[3])
    dims = (groups_x, groups_y, cells_x, cells_y, cells_z, per_peer)
    both = ("gx", "gy")
    width = -(-len(SIDES) * per_peer // LANES) * LANES
    vmem = pl.BlockSpec(memory_space=pltpu.VMEM)
    smem = pl.BlockSpec(memory_space=pltpu.SMEM)
    hbm = pl.BlockSpec(memory_space=pltpu.HBM)

    stored = jnp.transpose(velocity, (0, 2, 1, 3))

    def shifted(first, last, axis):
        peers = lax.axis_size(axis)
        up = [(i, (i + 1) % peers) for i in range(peers)]
        down = [(j, i) for i, j in up]
        return lax.ppermute(last, axis, up), lax.ppermute(first, axis, down)

    slab = (REACH, 3, cells_y, cells_z)
    x_first, x_last = pl.pallas_call(
        edge_kernel_x,
        out_shape=(jax.ShapeDtypeStruct(slab, BF16),) * 2,
        in_specs=[hbm],
        out_specs=(vmem,) * 2,
        scratch_shapes=[pltpu.VMEM((2,) + slab, F32), pltpu.SemaphoreType.DMA((2,))],
        compiler_params=pltpu.CompilerParams(vmem_limit_bytes=61 * MIB),
        name="edges_x",
    )(stored)
    x_low, x_high = shifted(x_first, x_last, "gx")
    payload = pl.pallas_call(
        functools.partial(front_kernel, dims),
        out_shape=jax.ShapeDtypeStruct((devices, 8, width), F32),
        in_specs=[smem] + [vmem] * 4,
        out_specs=vmem,
        scratch_shapes=[
            pltpu.VMEM((8, slots), F32),
            pltpu.VMEM((devices, 8, LANES), F32),
            pltpu.VMEM((8 * devices, LANES), F32),
            pltpu.VMEM((devices, 8, LANES), jnp.int32),
        ],
        compiler_params=pltpu.CompilerParams(vmem_limit_bytes=61 * MIB),
        name="points_out",
    )(counts, fiber_loads, fractions, corners, neighbours)
    received = lax.all_to_all(payload, both, split_axis=0, concat_axis=0, tiled=True)
    strip = (cells_x + 2 * REACH, 3, REACH, cells_z)
    y_first, y_last = pl.pallas_call(
        edge_kernel_y,
        out_shape=(jax.ShapeDtypeStruct(strip, BF16),) * 2,
        in_specs=[hbm] * 3,
        out_specs=(vmem,) * 2,
        scratch_shapes=[
            pltpu.VMEM((2, cells_x, 3, 8, cells_z), F32),
            pltpu.VMEM((2,) + slab, BF16),
            pltpu.SemaphoreType.DMA((4,)),
        ],
        compiler_params=pltpu.CompilerParams(vmem_limit_bytes=61 * MIB),
        name="edges_y",
    )(stored, x_low, x_high)
    y_low, y_high = shifted(y_first, y_last, "gy")

    block = min(slots, 1536)
    ext_x, ext_y, inner_x = cells_x + 2 * REACH, cells_y + 2 * REACH, cells_x + REACH
    side_rows = max((REACH + 2) * ext_y, inner_x * 16)
    field, back = pl.pallas_call(
        functools.partial(main_kernel, dims),
        out_shape=(
            jax.ShapeDtypeStruct(stored.shape, F32),
            jax.ShapeDtypeStruct((devices, 8, LANES), F32),
        ),
        in_specs=[vmem] + [hbm] * 5,
        out_specs=(hbm, vmem),
        scratch_shapes=[
            pltpu.VMEM((8, slots), F32),
            pltpu.VMEM((8, slots), F32),
            pltpu.VMEM((8, slots), F32),
            pltpu.VMEM((8, slots), F32),
            pltpu.VMEM((inner_x * ext_y, block), BF16),
            pltpu.VMEM((3, cells_z, block), BF16),
            pltpu.VMEM((cells_z, block), F32),
            pltpu.VMEM((2, side_rows, 256), BF16),
            pltpu.VMEM((2, 3, cells_z, 256), BF16),
            pltpu.VMEM((ext_x, 3, ext_y, cells_z), F32),
            pltpu.VMEM((ext_x, 3, ext_y, cells_z), F32),
            pltpu.VMEM((3, inner_x * ext_y, cells_z), BF16),
            pltpu.VMEM(stored.shape, F32),
            pltpu.VMEM((8, slots), F32),
            pltpu.VMEM((2,) + slab, BF16),
            pltpu.VMEM((2,) + strip, BF16),
            pltpu.SemaphoreType.DMA((6,)),
        ],
        compiler_params=pltpu.CompilerParams(vmem_limit_bytes=STEP_MIB * MIB),
        name="step",
    )(received, stored, x_low, x_high, y_low, y_high)
    returned = lax.all_to_all(back, both, split_axis=0, concat_axis=0, tiled=True)
    sampled = pl.pallas_call(
        functools.partial(last_kernel, per_peer),
        out_shape=jax.ShapeDtypeStruct((3, slots), F32),
        in_specs=[smem, vmem],
        out_specs=vmem,
        compiler_params=pltpu.CompilerParams(vmem_limit_bytes=12 * MIB),
        name="points_back",
    )(counts, returned)
    return (jnp.transpose(field, (0, 2, 1, 3)), sampled)


def solution(mesh):
    return jax.shard_map(
        staged,
        mesh=mesh,
        in_specs=(
            P("gx", "gy", None, None),
            P(None, ("gx", "gy")),
            P(None, ("gx", "gy")),
            P(None, ("gx", "gy")),
            P(("gx", "gy")),
            P(("gx", "gy")),
        ),
        out_specs=(P("gx", "gy", None, None), P(None, ("gx", "gy"))),
        check_vma=False,
    )
```

```python
import functools

import jax
import jax.numpy as jnp
from jax import lax
from jax.experimental import pallas as pl
from jax.experimental.pallas import tpu as pltpu
from jax.sharding import PartitionSpec as P


viscosity = 0.15
F32 = jnp.float32
BF16 = jnp.bfloat16
LANES = 128
MIB = 1024 * 1024
STEP_MIB = 58
REACH = 4

SIDES = ((-1, -1), (-1, 0), (-1, 1), (1, -1), (1, 0), (1, 1), (0, -1), (0, 1))


def iota(shape, dim):
    return lax.broadcasted_iota(jnp.int32, shape, dim)


def piece_at(tile_of, start, width, target):
    first, off = divmod(start, LANES)
    shift = (target - off) % LANES
    out = pltpu.roll(tile_of(first), shift, 1) if shift else tile_of(first)
    spill = off + width - LANES
    if spill > 0:
        rest = tile_of(first + 1)
        rest = pltpu.roll(rest, shift, 1) if shift else rest
        lane = iota(out.shape, 1)
        begin = (target + width - spill) % LANES
        end = begin + spill
        inside = (lane >= begin) & (lane < end)
        if end > LANES:
            inside = inside | (lane < end - LANES)
        out = jnp.where(inside, rest, out)
    return out


def lane_mask(shape, begin, end):
    lane = iota(shape, 1)
    return (lane >= begin) & (lane < end)


def front_kernel(dims, counts, loads, fractions, corners, neighbours, out, rows, buckets, reach, order):
    groups_x, groups_y, cells_x, cells_y, cells_z, per_peer = dims
    devices = groups_x * groups_y
    slots = loads.shape[1]
    tiles = slots // LANES
    whole_x, whole_y = groups_x * cells_x, groups_y * cells_y
    position = corners[...].astype(F32) + fractions[...]
    for c in range(3):
        rows[2 * c : 2 * c + 1, :] = loads[c : c + 1, :]
        rows[2 * c + 1 : 2 * c + 2, :] = position[c : c + 1, :]
    rows[6:8, :] = jnp.zeros((2, slots), F32)
    sub = iota((8, LANES), 0)
    lane = iota((8, LANES), 1)
    even = (sub % 2) == 0
    stiffness = jnp.where(sub == 1, 2.0 / whole_x, jnp.where(sub == 3, 2.0 / whole_y, 2.0 / cells_z))
    stiffness = jnp.where((sub % 2 == 1) & (sub < 6), stiffness, 0.0).astype(F32)

    def force(t, _):
        at = pl.ds(pl.multiple_of(t * LANES, LANES), LANES)
        index = jnp.broadcast_to(neighbours[at].reshape(1, LANES), (8, LANES))
        high, low = index // LANES, index % LANES
        here = rows[:, at]
        partner = jnp.zeros((8, LANES), F32)
        for h in range(tiles):
            picked = jnp.take_along_axis(rows[:, h * LANES : (h + 1) * LANES], low, axis=1)
            partner = jnp.where(high == h, picked, partner)
        pull = pltpu.roll(stiffness * (partner - here), 7, 0)
        rows[:, at] = jnp.where(even, here + pull, here)
        return 0

    lax.fori_loop(0, tiles, force, 0, unroll=4)

    far = 1.0e9
    low_x = sum([jnp.where(sub == k, cells_x - REACH - 3.0 if dx < 0 else -far, 0.0) for k, (dx, _) in enumerate(SIDES)])
    end_x = sum([jnp.where(sub == k, float(REACH) if dx > 0 else far, 0.0) for k, (dx, _) in enumerate(SIDES)])
    low_y = sum([jnp.where(sub == k, cells_y - REACH - 3.0 if dy < 0 else -far, 0.0) for k, (_, dy) in enumerate(SIDES)])
    end_y = sum([jnp.where(sub == k, float(REACH) if dy > 0 else far, 0.0) for k, (_, dy) in enumerate(SIDES)])
    period = jnp.where(sub == 1, float(whole_x), jnp.where(sub == 3, float(whole_y), 4.0e9)).astype(F32)
    for d in range(devices):
        a, b = divmod(d, groups_y)
        got = piece_at(lambda i: rows[:, i * LANES : (i + 1) * LANES], d * per_peer, per_peer, 0)
        base = jnp.where(sub == 1, float(a * cells_x), jnp.where(sub == 3, float(b * cells_y), 0.0)).astype(F32)
        moved = got - base
        moved = jnp.where(moved > 0.5 * period, moved - period, moved)
        moved = jnp.where(moved < -0.5 * period, moved + period, moved)
        live = lane < counts[d]
        local = jnp.where(live, jnp.where(even, got, moved), jnp.where(even | (lane >= per_peer), 0.0, moved))
        buckets[d] = local
        at_x = jnp.broadcast_to(local[1:2], (8, LANES))
        at_y = jnp.broadcast_to(local[3:4], (8, LANES))
        near = live & (at_x >= low_x) & (at_x < end_x) & (at_y >= low_y) & (at_y < end_y)
        reach[8 * d : 8 * d + 8, :] = jnp.where(near, 1.0, 0.0)

    before = jnp.where(iota((LANES, LANES), 0) <= iota((LANES, LANES), 1), 1.0, 0.0).astype(BF16)
    reach[...] = jnp.dot(reach[...].astype(BF16), before, preferred_element_type=F32)
    starts = sum([jnp.where(sub == k, (k * per_peer) % LANES, 0) for k in range(len(SIDES))])
    rank = ((lane - starts + LANES) % LANES).astype(F32)

    def find(d, _):
        upto = reach[pl.ds(pl.multiple_of(8 * d, 8), 8), :]
        spot = jnp.zeros((8, LANES), jnp.int32)
        for bit in (32, 16, 8, 4, 2, 1):
            seen = jnp.take_along_axis(upto, spot + (bit - 1), axis=1)
            spot = jnp.where(seen <= rank, spot + bit, spot)
        order[d] = spot
        return 0

    lax.fori_loop(0, devices, find, 0, unroll=16)
    tiles_out = out.shape[2] // LANES

    def send(d):
        a, b = divmod(d, groups_y)
        acc = [jnp.zeros((8, LANES), F32) for _ in range(tiles_out)]

        def put(value, start, rows_ok):
            m, off = divmod(start, LANES)
            ok = lane_mask((8, LANES), off, min(off + per_peer, LANES))
            ok = ok if rows_ok is None else ok & rows_ok
            acc[m] = jnp.where(ok, value, acc[m])
            if off + per_peer > LANES:
                ok = lane_mask((8, LANES), 0, off + per_peer - LANES)
                ok = ok if rows_ok is None else ok & rows_ok
                acc[m + 1] = jnp.where(ok, value, acc[m + 1])

        counted = []
        for k, (dx, dy) in enumerate(SIDES):
            owner = ((a + dx + groups_x) % groups_x) * groups_y + (b + dy + groups_y) % groups_y
            index = jnp.broadcast_to(order[owner, k : k + 1, :], (8, LANES))
            put(jnp.take_along_axis(buckets[owner], index, axis=1), k * per_peer, None)
            counted.append(jnp.broadcast_to(reach[8 * owner + k : 8 * owner + k + 1, :], (8, LANES)))
        own = buckets[d]
        for c in range(3):
            value = pltpu.roll(own, 6 - 2 * c, 0)
            value = pltpu.roll(value, (c * per_peer) % LANES, 1) if c else value
            put(value, c * per_peer, sub >= 6)
        for k, count in enumerate(counted):
            acc[-1] = jnp.where((sub == 7) & (lane == LANES - 8 + k), count, acc[-1])
        for m in range(tiles_out):
            out[d, :, m * LANES : (m + 1) * LANES] = acc[m]

    for d in range(devices):
        send(d)


def quarter_sine(t):
    half_pi = 1.5707963267948966
    coeffs = []
    term = half_pi
    for n in range(8):
        coeffs.append(term)
        term = -term * half_pi * half_pi / ((2 * n + 2) * (2 * n + 3))
    square = t * t
    total = jnp.full_like(t, coeffs[-1])
    for coeff in coeffs[-2::-1]:
        total = total * square + coeff
    return total * t


def main_kernel(
    dims, got, velocity, x_low_in, x_high_in, y_low_in, y_high_in, field, back,
    own, floors, sines, cosines, wts, push, depth, side_wts, side_push, grid, mid, rounded, own_vel, values, x_sides, y_sides, sems,
):
    groups_x, groups_y, cells_x, cells_y, cells_z, per_peer = dims
    sources = groups_x * groups_y
    points = sources * per_peer
    block = wts.shape[1]
    blocks = points // block
    ext_x, ext_y = cells_x + 2 * REACH, cells_y + 2 * REACH
    inner_x = cells_x + REACH
    load_vel = pltpu.make_async_copy(velocity, own_vel, sems.at[0])
    load_vel.start()
    load_sides = []
    for i, ref in enumerate((x_low_in, x_high_in, y_low_in, y_high_in)):
        to = (x_sides if i < 2 else y_sides).at[i % 2]
        load_sides.append(pltpu.make_async_copy(ref, to, sems.at[2 + i]))
        load_sides[-1].start()
    sub = iota((8, LANES), 0)
    lane = iota((8, LANES), 1)

    for m in range(points // LANES):
        acc = jnp.zeros((8, LANES), F32)
        for s in range(m * LANES // per_peer, -(-(m + 1) * LANES // per_peer)):
            at = s * per_peer - m * LANES
            ok = lane_mask((8, LANES), max(at, 0), min(at + per_peer, LANES))
            for c in range(3):
                value = piece_at(lambda i, s=s: got[s, :, i * LANES : (i + 1) * LANES], c * per_peer, per_peer, at % LANES)
                value = pltpu.roll(value, (2 * c - 6) % 8, 0)
                acc = jnp.where(ok & (sub // 2 == c), value, acc)
        own[:, m * LANES : (m + 1) * LANES] = acc

    def split(position):
        floor = jnp.floor(position)
        fraction = position - floor
        return floor, quarter_sine(fraction), quarter_sine(1.0 - fraction)

    floors[...], sines[...], cosines[...] = split(own[...])

    def weights(s, co):
        return (0.25 * (1.0 - s), 0.25 * (1.0 + co), 0.25 * (1.0 + s), 0.25 * (1.0 - co))

    def table(coordinate, cells, wt):
        out = jnp.zeros(jnp.broadcast_shapes(coordinate.shape, cells[0].shape), F32)
        for cell, w in zip(cells, wt):
            out = jnp.where(coordinate == cell, w, out)
        return out

    def coord(rows, lanes, f):
        return f(iota((rows, lanes), 0)).astype(F32)

    def along(cell, wt, rows, rule):
        return table(coord(rows, cell.shape[1], rule), [cell + float(i) for i in range(4)], wt)

    def push_rows(cell, wt, forces, to_push, to, keep):
        lanes = cell.shape[1]
        cells = []
        for i in range(4):
            moved = cell + float(i)
            cells.append(jnp.where(moved >= float(cells_z), moved - float(cells_z), moved))
        step = 64
        for z in range(0, cells_z, step):
            part = table(coord(step, lanes, lambda r: r + z), cells, wt)
            if keep:
                depth[z : z + step, to] = part
            for c in range(3):
                to_push[c, z : z + step, to] = (part * forces[c]).astype(BF16)

    def circle(r):
        return jnp.where(r < cells_y + REACH, r, r - ext_y)

    def pair_rows(ax, ay, x):
        return jnp.concatenate([ax[x : x + 1] * ay, ax[x + 1 : x + 2] * ay], axis=0).astype(BF16)

    chunk = 256

    def build_own(base):
        def step(i, _):
            at = pl.ds(pl.multiple_of(base + i * chunk, chunk), chunk)
            to = pl.ds(pl.multiple_of(i * chunk, chunk), chunk)
            cell = [floors[2 * c + 1 : 2 * c + 2, at] for c in range(3)]
            wt = [weights(sines[2 * c + 1 : 2 * c + 2, at], cosines[2 * c + 1 : 2 * c + 2, at]) for c in range(3)]
            ax = along(cell[0], wt[0], -(-inner_x // 8) * 8, lambda r: r - 2)
            ay = along(cell[1], wt[1], ext_y, circle)
            for x in range(0, inner_x, 2):
                wts[x * ext_y : (x + 2) * ext_y, to] = pair_rows(ax, ay, x)
            push_rows(cell[2], wt[2], [own[2 * c : 2 * c + 1, at] for c in range(3)], push, to, True)
            return 0

        lax.fori_loop(0, block // chunk, step, 0)

    def dot_t(a, b):
        return lax.dot_general(a, b, (((1,), (1,)), ((), ())), preferred_element_type=F32)

    edge = REACH + 2
    together = chunk // 8
    rounds = sources // together
    most = got[0, :, got.shape[2] - LANES :]
    for s in range(1, sources):
        most = jnp.maximum(most, got[s, :, got.shape[2] - LANES :])
    counts = [
        jnp.max(jnp.where((sub == 7) & (lane == LANES - 8 + k), most, 0.0)).astype(jnp.int32) for k in range(len(SIDES))
    ]

    def side(it, slot, k, dx, dy):
        first = -REACH if dx < 0 else cells_x - 2
        start = k * per_peer + (it // rounds if rounds > 1 else it) * 8
        source = (it % rounds if rounds > 1 else 0) * together
        at = pl.ds(pl.multiple_of(start // LANES * LANES, LANES), LANES)
        off = start % LANES
        parts = []
        for m in range(chunk // LANES):
            acc = jnp.zeros((8, LANES), F32)
            for i in range(LANES // 8):
                value = pltpu.roll(got[source + m * (LANES // 8) + i, :, at], (8 * i - off + LANES) % LANES, 1)
                acc = jnp.where(lane // 8 == i, value, acc)
            parts.append(acc)
        data = jnp.concatenate(parts, axis=1)
        floor, sine, cosine = split(data)
        cell = [floor[2 * c + 1 : 2 * c + 2] for c in range(3)]
        cell[0] = cell[0] + float(dx * cells_x)
        cell[1] = cell[1] + jnp.asarray(dy * cells_y).astype(F32)
        wt = [weights(sine[2 * c + 1 : 2 * c + 2], cosine[2 * c + 1 : 2 * c + 2]) for c in range(3)]
        if dx:
            ax = along(cell[0], wt[0], 8, lambda r: r + first)
            ay = along(cell[1], wt[1], ext_y, circle)
            for x in range(0, edge, 2):
                side_wts[slot, x * ext_y : (x + 2) * ext_y, :] = pair_rows(ax, ay, x)
        else:
            tile_a = 0 if dy < 0 else cells_y - 8
            ax = along(cell[0], wt[0], -(-inner_x // 8) * 8, lambda r: r - 2)
            ay = along(cell[1], wt[1], 16, lambda r: circle(jnp.where(r < 8, r + tile_a, r - 8 + cells_y)))
            for x in range(inner_x):
                side_wts[slot, x * 16 : (x + 1) * 16, :] = (ax[x : x + 1] * ay).astype(BF16)
        push_rows(cell[2], wt[2], [data[2 * c : 2 * c + 1] for c in range(3)], side_push.at[slot], slice(None), False)

    def side_sum(slot, k):
        dx, dy = SIDES[k]
        first = -REACH if dx < 0 else cells_x - 2
        tile_a = 0 if dy < 0 else cells_y - 8
        for c in range(3):
            if dx:
                total = dot_t(side_wts[slot, 0 : edge * ext_y, :], side_push[slot, c]).reshape(edge, ext_y, cells_z)
                grid[first + REACH : first + REACH + edge, c] += total
            else:
                total = dot_t(side_wts[slot, 0 : inner_x * 16, :], side_push[slot, c]).reshape(inner_x, 2, 8, cells_z)
                grid[2 : 2 + inner_x, c, tile_a : tile_a + 8] += total[:, 0]
                grid[2 : 2 + inner_x, c, cells_y : cells_y + 8] += total[:, 1]

    for base in range(0, points, block):
        build_own(base)
        if base == 0:
            load_vel.wait()

        def spread_own(c, _, base=base):
            if base == 0:
                side(0, 2 * c, c, -1, c - 1)
                side(0, 2 * c + 1, c + 3, 1, c - 1)
            total = dot_t(wts[...], push[c]).reshape(inner_x, ext_y, cells_z)
            if base == 0:
                grid[2 : 2 + inner_x, c] = total
                grid[0:2, c] = jnp.zeros((2, ext_y, cells_z), F32)
                grid[2 + inner_x :, c] = jnp.zeros((2, ext_y, cells_z), F32)
                grid[REACH : REACH + cells_x, c, 0:cells_y] = total[2 : 2 + cells_x, 0:cells_y] + own_vel[:, c]
            else:
                grid[2 : 2 + inner_x, c] += total
            return 0

        lax.fori_loop(0, 3, spread_own, 0)

    pairs = ((0, 3), (1, 4), (2, 5), (6, 7))
    side(0, 6, 6, 0, -1)
    side(0, 7, 7, 0, 1)
    for i, pair in enumerate(pairs):
        for j, k in enumerate(pair):
            side_sum(2 * i + j, k)
    for pair in pairs:

        def both(it, _, pair=pair):
            for j, k in enumerate(pair):
                side(it, j, k, *SIDES[k])
            for j, k in enumerate(pair):
                side_sum(j, k)
            return 0

        most_of = jnp.maximum(counts[pair[0]], counts[pair[1]])
        lax.fori_loop(1, (most_of + 7) // 8 * rounds, both, 0)

    for copy in load_sides:
        copy.wait()
    (x_low, x_high), (y_low, y_high) = (x_sides.at[0], x_sides.at[1]), (y_sides.at[0], y_sides.at[1])

    def add_edges(x, _):
        for c in range(3):
            grid[x, c, 0:cells_y] += x_low[x, c].astype(F32)
            grid[x + REACH + cells_x, c, 0:cells_y] += x_high[x, c].astype(F32)
        return 0

    lax.fori_loop(0, REACH, add_edges, 0)

    def add_sides(x, _):
        for c in range(3):
            pair = jnp.concatenate([y_high[x, c].astype(F32), y_low[x, c].astype(F32)], axis=0)
            grid[x, c, cells_y:ext_y] += pair
        return 0

    lax.fori_loop(0, ext_x, add_sides, 0, unroll=2)

    center_wt = (1.0 - 6.0 * viscosity) / viscosity

    eight = iota((8, cells_z), 0)

    def swept(ref, x, c):
        tiles = [ref[x, c, i : i + 8, :] for i in range(0, ext_y, 8)]
        ups = [pltpu.roll(tile, 1, 0) for tile in tiles]
        downs = [pltpu.roll(tile, 7, 0) for tile in tiles]
        out = []
        for i, tile in enumerate(tiles):
            at = slice(8 * i, 8 * i + 8)
            total = ref[x - 1, c, at, :] + ref[x + 1, c, at, :]
            total = total + jnp.where(eight == 0, ups[i - 1], ups[i])
            total = total + jnp.where(eight == 7, downs[(i + 1) % len(tiles)], downs[i])
            total = total + pltpu.roll(tile, 1, 1) + pltpu.roll(tile, cells_z - 1, 1)
            out.append(center_wt * tile + total)
        return jnp.concatenate(out, axis=0)

    def first_sweep(i, _):
        for x in range(4):
            for c in range(3):
                mid[1 + 4 * i + x, c] = swept(grid, 1 + 4 * i + x, c)
        return 0

    lax.fori_loop(0, (ext_x - 2) // 4, first_sweep, 0)
    for x in range((ext_x - 2) // 4 * 4 + 1, ext_x - 1):
        for c in range(3):
            mid[x, c] = swept(grid, x, c)

    def second_sweep(i, _):
        for j in range(2):
            at_x = 2 + 4 * i + 2 * j
            for c in range(3):
                two = [viscosity * viscosity * swept(mid, at_x + x, c) for x in range(2)]
                grid[at_x, c] = two[0]
                grid[at_x + 1, c] = two[1]
                at = pl.ds(pl.multiple_of((2 * i + j) * 2 * ext_y, 2 * ext_y), 2 * ext_y)
                rounded[c, at, :] = jnp.concatenate(two, axis=0).astype(BF16)
        return 0

    lax.fori_loop(0, inner_x // 4, second_sweep, 0)
    store = pltpu.make_async_copy(grid.at[REACH : REACH + cells_x, :, 0:cells_y, :], field, sems.at[1])
    store.start()

    values[3:8, :] = jnp.zeros((5, points), F32)
    for base in range(0, points, block):
        if blocks > 1:
            build_own(base)
        for c in range(3):
            mixed = lax.dot_general(rounded[c], wts[...], (((0,), (0,)), ((), ())), preferred_element_type=F32)
            values[c : c + 1, base : base + block] = jnp.sum(mixed * depth[...], axis=0, keepdims=True)
    for s in range(sources):
        back[s] = piece_at(lambda i: values[:, i * LANES : (i + 1) * LANES], s * per_peer, per_peer, 0)[0:4]
    store.wait()


def edge_kernel_x(stored, out_first, out_last, held, sems):
    cells_x = stored.shape[0]
    copies = []
    for i, at in enumerate((0, cells_x - REACH)):
        copies.append(pltpu.make_async_copy(stored.at[at : at + REACH], held.at[i], sems.at[i]))
        copies[-1].start()
    for i, out in enumerate((out_first, out_last)):
        copies[i].wait()
        out[...] = held[i].astype(BF16)


def edge_kernel_y(stored, x_low, x_high, out_first, out_last, held, sides, sems):
    cells_x, cells_y = stored.shape[0], stored.shape[2]
    copies = []
    for i, at in enumerate((0, cells_y - 8)):
        copies.append(pltpu.make_async_copy(stored.at[:, :, at : at + 8, :], held.at[i], sems.at[i]))
    for i, ref in enumerate((x_low, x_high)):
        copies.append(pltpu.make_async_copy(ref, sides.at[i], sems.at[2 + i]))
    for copy in copies:
        copy.start()
    for copy in copies:
        copy.wait()
    out_first[REACH : REACH + cells_x] = held[0, :, :, 0:REACH].astype(BF16)
    out_last[REACH : REACH + cells_x] = held[1, :, :, 8 - REACH :].astype(BF16)
    for i, at in enumerate((0, REACH + cells_x)):
        out_first[at : at + REACH] = sides[i, :, :, 0:8].astype(F32)[:, :, 0:REACH].astype(BF16)
        out_last[at : at + REACH] = sides[i, :, :, cells_y - 8 :].astype(F32)[:, :, 8 - REACH :].astype(BF16)


def last_kernel(per_peer, counts, got, out):
    for m in range(out.shape[1] // LANES):
        acc = jnp.zeros((4, LANES), F32)
        for s in range(m * LANES // per_peer, -(-(m + 1) * LANES // per_peer)):
            at = s * per_peer - m * LANES
            lane = iota((4, LANES), 1)
            ok = (lane >= max(at, 0)) & (lane < jnp.minimum(at + counts[s], min(at + per_peer, LANES)))
            value = got[s]
            value = pltpu.roll(value, at % LANES, 1) if at % LANES else value
            acc = jnp.where(ok, value, acc)
        out[:, m * LANES : (m + 1) * LANES] = acc[0:3]


def staged(velocity, fiber_loads, fractions, corners, neighbours, counts):
    groups_x = lax.axis_size("gx")
    groups_y = lax.axis_size("gy")
    devices = groups_x * groups_y
    slots = fiber_loads.shape[1]
    per_peer = slots // devices
    cells_x, cells_y, cells_z = (velocity.shape[0], velocity.shape[1], velocity.shape[3])
    dims = (groups_x, groups_y, cells_x, cells_y, cells_z, per_peer)
    both = ("gx", "gy")
    width = -(-len(SIDES) * per_peer // LANES) * LANES
    vmem = pl.BlockSpec(memory_space=pltpu.VMEM)
    smem = pl.BlockSpec(memory_space=pltpu.SMEM)
    hbm = pl.BlockSpec(memory_space=pltpu.HBM)

    stored = jnp.transpose(velocity, (0, 2, 1, 3))

    def shifted(first, last, axis):
        peers = lax.axis_size(axis)
        up = [(i, (i + 1) % peers) for i in range(peers)]
        down = [(j, i) for i, j in up]
        return lax.ppermute(last, axis, up), lax.ppermute(first, axis, down)

    slab = (REACH, 3, cells_y, cells_z)
    x_first, x_last = pl.pallas_call(
        edge_kernel_x,
        out_shape=(jax.ShapeDtypeStruct(slab, BF16),) * 2,
        in_specs=[hbm],
        out_specs=(vmem,) * 2,
        scratch_shapes=[pltpu.VMEM((2,) + slab, F32), pltpu.SemaphoreType.DMA((2,))],
        compiler_params=pltpu.CompilerParams(vmem_limit_bytes=61 * MIB),
        name="edges_x",
    )(stored)
    x_low, x_high = shifted(x_first, x_last, "gx")
    payload = pl.pallas_call(
        functools.partial(front_kernel, dims),
        out_shape=jax.ShapeDtypeStruct((devices, 8, width), F32),
        in_specs=[smem] + [vmem] * 4,
        out_specs=vmem,
        scratch_shapes=[
            pltpu.VMEM((8, slots), F32),
            pltpu.VMEM((devices, 8, LANES), F32),
            pltpu.VMEM((8 * devices, LANES), F32),
            pltpu.VMEM((devices, 8, LANES), jnp.int32),
        ],
        compiler_params=pltpu.CompilerParams(vmem_limit_bytes=61 * MIB),
        name="points_out",
    )(counts, fiber_loads, fractions, corners, neighbours)
    received = lax.all_to_all(payload, both, split_axis=0, concat_axis=0, tiled=True)
    strip = (cells_x + 2 * REACH, 3, REACH, cells_z)
    y_first, y_last = pl.pallas_call(
        edge_kernel_y,
        out_shape=(jax.ShapeDtypeStruct(strip, BF16),) * 2,
        in_specs=[hbm] * 3,
        out_specs=(vmem,) * 2,
        scratch_shapes=[
            pltpu.VMEM((2, cells_x, 3, 8, cells_z), F32),
            pltpu.VMEM((2,) + slab, BF16),
            pltpu.SemaphoreType.DMA((4,)),
        ],
        compiler_params=pltpu.CompilerParams(vmem_limit_bytes=61 * MIB),
        name="edges_y",
    )(stored, x_low, x_high)
    y_low, y_high = shifted(y_first, y_last, "gy")

    block = min(slots, 1536)
    ext_x, ext_y, inner_x = cells_x + 2 * REACH, cells_y + 2 * REACH, cells_x + REACH
    side_rows = max((REACH + 2) * ext_y, inner_x * 16)
    field, back = pl.pallas_call(
        functools.partial(main_kernel, dims),
        out_shape=(
            jax.ShapeDtypeStruct(stored.shape, F32),
            jax.ShapeDtypeStruct((devices, 4, LANES), F32),
        ),
        in_specs=[vmem] + [hbm] * 5,
        out_specs=(hbm, vmem),
        scratch_shapes=[
            pltpu.VMEM((8, slots), F32),
            pltpu.VMEM((8, slots), F32),
            pltpu.VMEM((8, slots), F32),
            pltpu.VMEM((8, slots), F32),
            pltpu.VMEM((inner_x * ext_y, block), BF16),
            pltpu.VMEM((3, cells_z, block), BF16),
            pltpu.VMEM((cells_z, block), F32),
            pltpu.VMEM((8, side_rows, 256), BF16),
            pltpu.VMEM((8, 3, cells_z, 256), BF16),
            pltpu.VMEM((ext_x, 3, ext_y, cells_z), F32),
            pltpu.VMEM((ext_x, 3, ext_y, cells_z), F32),
            pltpu.VMEM((3, inner_x * ext_y, cells_z), BF16),
            pltpu.VMEM(stored.shape, F32),
            pltpu.VMEM((8, slots), F32),
            pltpu.VMEM((2,) + slab, BF16),
            pltpu.VMEM((2,) + strip, BF16),
            pltpu.SemaphoreType.DMA((6,)),
        ],
        compiler_params=pltpu.CompilerParams(vmem_limit_bytes=STEP_MIB * MIB),
        name="step",
    )(received, stored, x_low, x_high, y_low, y_high)
    returned = lax.all_to_all(back, both, split_axis=0, concat_axis=0, tiled=True)
    sampled = pl.pallas_call(
        functools.partial(last_kernel, per_peer),
        out_shape=jax.ShapeDtypeStruct((3, slots), F32),
        in_specs=[smem, vmem],
        out_specs=vmem,
        compiler_params=pltpu.CompilerParams(vmem_limit_bytes=12 * MIB),
        name="points_back",
    )(counts, returned)
    return (jnp.transpose(field, (0, 2, 1, 3)), sampled)


def solution(mesh):
    return jax.shard_map(
        staged,
        mesh=mesh,
        in_specs=(
            P("gx", "gy", None, None),
            P(None, ("gx", "gy")),
            P(None, ("gx", "gy")),
            P(None, ("gx", "gy")),
            P(("gx", "gy")),
            P(("gx", "gy")),
        ),
        out_specs=(P("gx", "gy", None, None), P(None, ("gx", "gy"))),
        check_vma=False,
    )
```
